256 devices in a mesh: seq: 32 (over x, y, core), tp: 8 (over z).
Axes of the slice: x: 4, y: 4, z: 8, core: 2. Of those that a mesh axis runs over, the one named last changes fastest.
Arguments:
- queries: bfloat16 [49152, 4096], P(('seq', 'tp')), may hold values from -9 to 9
- keys_values: bfloat16 [49152, 2048], P(('seq', 'tp')), may hold values from -8 to 8
- doc_lengths: int32 [32], replicated, may hold values from 1 to 3072, 49152 in all
- block_target: int32 [384], replicated, may hold values from 0 to 31, as said below
Outputs:
- attention_output: bfloat16 [49152, 4096], P('seq', 'tp')
The draws below stay inside these ranges and needn't reach their ends.
Inputs may be any that keep to these rules, and one draw needn't show every extreme that they name: `doc_lengths`: the lengths add up to 49152, and the largest is exactly 3072. `block_target`: every shard of seq is named by exactly 12 blocks, and the 12 blocks of one shard of seq (blocks k * 12 to k * 12 + 11) name no shard more than 1 times, some shard exactly 1 times.
All inputs are finite; a program needn't handle non-finite values.
Results may differ from the reference program's by a relative error of at most 0.0036.
Values may be sent and summed in bfloat16 or wider, within the bound.
A program may use at most 128 MiB of HBM per device.

```python
import math
import jax
import jax.numpy as jnp
import numpy as np
from jax import lax

HEADS = 32
KV_HEADS = 8
HEAD = 128
BLOCK = 128
MAXDOC = 3072
TOKENS = 49152
BLK_DEV = 12
BLOCKS = 384
DOCS = 32
N_SEQ = 32


def field_pair(key):
    head_group = HEADS // KV_HEADS
    query_field = jnp.clip(1.5 * jax.random.normal(jax.random.fold_in(key, 23), (TOKENS, KV_HEADS, head_group, HEAD)), -9.0, 9.0)
    pair_field = jnp.clip(jax.random.normal(jax.random.fold_in(key, 24), (TOKENS, KV_HEADS, 2, HEAD)), -6.0, 6.0)
    return (query_field.reshape(TOKENS, HEADS * HEAD), pair_field.reshape(TOKENS, KV_HEADS * 2 * HEAD))


def draw_queries(key, part):
    return field_pair(key)[0].astype(jnp.bfloat16)


def draw_keys_values(key, part):
    return field_pair(key)[1].astype(jnp.bfloat16)


def draw_block_target(key, part):
    block_ids = jnp.arange(BLOCKS, dtype=jnp.int32)
    loader = block_ids // BLK_DEV
    slot_ids = block_ids % BLK_DEV
    loader_shift = jax.random.permutation(jax.random.fold_in(key, 31), N_SEQ).astype(jnp.int32)
    slot_order = jax.random.permutation(jax.random.fold_in(key, 32), BLK_DEV).astype(jnp.int32)
    relabel = jax.random.permutation(jax.random.fold_in(key, 33), N_SEQ).astype(jnp.int32)
    rotated = (loader_shift[loader] + slot_order[slot_ids]) % N_SEQ
    return relabel[rotated].astype(jnp.int32)


def length_profile(number_of, total, bound, skew):
    loads = [(1 << 20) // math.isqrt(standing ** skew) + 1 for standing in range(2, number_of + 1)]
    rest, holding = total - bound - (number_of - 1), [1] * (number_of - 1)
    while rest > 0:
        candidates = [i for i in range(number_of - 1) if holding[i] < bound]
        whole, budget = sum([loads[i] for i in candidates]), rest
        for i in candidates:
            more = min(bound - holding[i], max(1, budget * loads[i] // whole), rest)
            holding[i] = holding[i] + more
            rest = rest - more
    return np.array([bound] + holding)


def ragged_sizes(stream_key, count, total, reach, skew):
    if count == 2:
        one = jax.random.randint(stream_key, (), max(1, total - reach), min(reach, total - 1) + 1)
        return jnp.stack([one, total - one])
    lengths = jnp.asarray(length_profile(count, total, reach, skew), jnp.int32)
    pairs = (count - 1) // 2
    source_of, receiver = lengths[1:1 + 2 * pairs:2], lengths[2:2 + 2 * pairs:2]
    room = jnp.minimum(source_of - 1, reach - receiver)
    shifted = jax.random.randint(jax.random.fold_in(stream_key, 1), (pairs,), 0, 1 << 20) % (room + 1)
    lengths = lengths.at[1:1 + 2 * pairs:2].set(source_of - shifted).at[2:2 + 2 * pairs:2].set(receiver + shifted)
    return lengths[jax.random.permutation(jax.random.fold_in(stream_key, 2), count)]


def setup_inputs(seed: int = 0) -> dict:
    arg_keys = jax.random.split(jax.random.key(seed), 5)
    return {
        "queries": draw_queries(jax.random.fold_in(arg_keys[4], 71), 0),
        "keys_values": draw_keys_values(jax.random.fold_in(arg_keys[4], 71), 0),
        "doc_lengths": ragged_sizes(arg_keys[2], DOCS, TOKENS, MAXDOC, 2).astype(jnp.int32),
        "block_target": draw_block_target(jax.random.fold_in(arg_keys[4], 71), 0),
    }


floor_score = -1e+30

def document_of(starts, positions):
    return lax.optimization_barrier(jnp.sum((positions[..., None] >= starts).astype(jnp.int32), axis=-1)) - 1

def reference(queries, keys_values, doc_lengths, block_target):
    starts = (jnp.cumsum(doc_lengths) - doc_lengths).astype(jnp.int32)
    head_group = HEADS // KV_HEADS
    block_total = TOKENS // BLOCK
    tile_total = MAXDOC // BLOCK + 1
    window = MAXDOC + BLOCK
    query_blocks = queries.reshape(block_total, BLOCK, KV_HEADS, head_group, HEAD)
    key_pairs = keys_values.reshape(TOKENS, KV_HEADS, 2, HEAD)
    padded = jnp.concatenate([jnp.zeros((MAXDOC, KV_HEADS, 2, HEAD), key_pairs.dtype), key_pairs], axis=0)
    factor = 1.0 / math.sqrt(HEAD)
    offsets = jnp.arange(BLOCK, dtype=jnp.int32)
    window_offsets = jnp.arange(window, dtype=jnp.int32)

    def one_block(block_index):
        query_first = (block_index * BLOCK).astype(jnp.int32)
        query_rows = lax.dynamic_index_in_dim(query_blocks, block_index, 0, keepdims=False).astype(jnp.float32)
        query_pos = query_first + offsets
        query_doc = document_of(starts, query_pos)
        chosen = lax.dynamic_slice_in_dim(padded, query_first.astype(jnp.int32), window, 0).astype(jnp.float32)
        key_pos = query_first - MAXDOC + window_offsets
        allowed = (document_of(starts, key_pos)[None, :] == query_doc[:, None]) & (key_pos[None, :] <= query_pos[:, None])
        actives = []
        pieces = []
        for tile_index in range(tile_total):
            key_first = query_first - MAXDOC + tile_index * BLOCK
            key_last = jnp.minimum(key_first + BLOCK - 1, query_first)
            active = document_of(starts, key_last) == query_doc[0]
            tile_keys = chosen[tile_index * BLOCK:(tile_index + 1) * BLOCK, :, 0]
            pieces.append(lax.cond(active, lambda keys_tile: jnp.einsum('qhgd,khd->hgqk', query_rows, keys_tile), lambda keys_tile: jnp.full((KV_HEADS, head_group, BLOCK, BLOCK), floor_score, jnp.float32), tile_keys))
            actives.append(active)
        scores = jnp.where(allowed, jnp.concatenate(pieces, axis=-1) * factor, floor_score)
        row_max = lax.optimization_barrier(jnp.max(scores, axis=-1, keepdims=True))
        exponents = jnp.where(allowed, jnp.exp(scores - row_max), 0.0)
        totals = lax.optimization_barrier(jnp.sum(exponents, axis=-1))
        weights = lax.optimization_barrier(exponents.astype(jnp.bfloat16)).astype(jnp.float32)
        accumulated = jnp.zeros((KV_HEADS, head_group, BLOCK, HEAD), jnp.float32)
        for tile_index in range(tile_total):
            tile_weights = weights[:, :, :, tile_index * BLOCK:(tile_index + 1) * BLOCK]
            tile_values = chosen[tile_index * BLOCK:(tile_index + 1) * BLOCK, :, 1]
            accumulated = accumulated + lax.cond(actives[tile_index], lambda operands: jnp.einsum('hgqk,khd->hgqd', operands[0], operands[1]), lambda operands: jnp.zeros((KV_HEADS, head_group, BLOCK, HEAD), jnp.float32), (tile_weights, tile_values))
        result = accumulated / totals[..., None]
        return jnp.transpose(result, (2, 0, 1, 3)).reshape(BLOCK, HEADS * HEAD).astype(jnp.bfloat16)
    attended = lax.map(one_block, jnp.arange(block_total, dtype=jnp.int32))
    block_order = jnp.argsort(block_target * block_total + jnp.arange(block_total, dtype=jnp.int32))
    return jnp.take(attended, block_order, axis=0).reshape(TOKENS, HEADS * HEAD)
```

```python
import functools
import math

import jax
import jax.numpy as jnp
from jax import lax
from jax.experimental import pallas as pl
from jax.experimental.pallas import tpu as pltpu
from jax.sharding import PartitionSpec as P

HEADS = 32
KV_HEADS = 8
HEAD = 128
BLOCK = 128
MAXDOC = 3072
DOCS = 32

MESH = pl.DeviceIdType.MESH
GROUP = HEADS // KV_HEADS
WIDTH = GROUP * HEAD
PAIR = 2 * HEAD
STEP_KEYS = 5 * BLOCK
WINDOW = MAXDOC + BLOCK
STEPS = WINDOW // STEP_KEYS
APART = -32768.0
SCALE = math.log2(math.e) / math.sqrt(HEAD)


def ring_order(n):
    order = []
    for d in range(1, n // 2 + 1):
        order.append(d)
        if n - d != d:
            order.append(n - d)
    return order


def gather_kernel(
    n_tp, n_seq, rows, q_ref, kv_ref, q_out, kv_out, kv_send, kv_recv, q_send, q_recv, h_send, h_recv, own_sem
):
    me = lax.axis_index("tp")
    shard = lax.axis_index("seq")
    shard_rows = n_tp * rows
    halo = MAXDOC // shard_rows
    order = ring_order(n_tp)

    barrier = pltpu.get_barrier_semaphore()
    for d in order:
        pl.semaphore_signal(barrier, inc=1, device_id={"tp": lax.rem(me + d, n_tp)}, device_id_type=MESH)
    for h in range(1, halo + 1):
        for s in (h, n_seq - h):
            pl.semaphore_signal(barrier, inc=1, device_id={"seq": lax.rem(shard + s, n_seq)}, device_id_type=MESH)
    pl.semaphore_wait(barrier, n_tp - 1 + 2 * halo)

    def columns(ref, which, width):
        return ref.at[:, pl.ds(pl.multiple_of(which * width, width), width)]

    def token_rows(ref, base, which):
        return ref.at[pl.ds(pl.multiple_of(base + which * rows, 64), rows), :]

    own_kv = pltpu.make_async_copy(columns(kv_ref, me, PAIR), token_rows(kv_out, MAXDOC, me), own_sem.at[0])
    own_q = pltpu.make_async_copy(columns(q_ref, me, WIDTH), token_rows(q_out, 0, me), own_sem.at[1])
    own_kv.start()
    kv_copies = {}
    for d in order:
        peer = lax.rem(me + d, n_tp)
        kv_copies[d] = pltpu.make_async_remote_copy(
            src_ref=columns(kv_ref, peer, PAIR),
            dst_ref=token_rows(kv_out, MAXDOC, me),
            send_sem=kv_send.at[d],
            recv_sem=kv_recv.at[d],
            device_id={"tp": peer},
            device_id_type=MESH,
        )
        kv_copies[d].start()
    q_copies = {}
    for d in order:
        peer = lax.rem(me + d, n_tp)
        q_copies[d] = pltpu.make_async_remote_copy(
            src_ref=columns(q_ref, peer, WIDTH),
            dst_ref=token_rows(q_out, 0, me),
            send_sem=q_send.at[d],
            recv_sem=q_recv.at[d],
            device_id={"tp": peer},
            device_id_type=MESH,
        )
        q_copies[d].start()
    own_q.start()

    halo_copies = []

    def relay(d):
        origin = lax.rem(me + n_tp - d, n_tp)
        for h in range(1, halo + 1):
            copy = pltpu.make_async_remote_copy(
                src_ref=token_rows(kv_out, MAXDOC, origin),
                dst_ref=token_rows(kv_out, MAXDOC - h * shard_rows, origin),
                send_sem=h_send.at[h - 1, d],
                recv_sem=h_recv.at[h - 1, d],
                device_id={"seq": lax.rem(shard + h, n_seq)},
                device_id_type=MESH,
            )
            copy.start()
            halo_copies.append(copy)

    own_kv.wait()
    relay(0)
    for d in order:
        kv_copies[d].wait_recv()
        relay(d)
    for d in order:
        kv_copies[d].wait_send()
    own_q.wait()
    for d in order:
        q_copies[d].wait()
    for copy in halo_copies:
        copy.wait()


def gather(queries, keys_values):
    n_tp, n_seq = lax.axis_size("tp"), lax.axis_size("seq")
    rows = queries.shape[0]
    halo = MAXDOC // (n_tp * rows)
    hbm = pl.BlockSpec(memory_space=pl.ANY)
    dma = pltpu.SemaphoreType.DMA
    return pl.pallas_call(
        functools.partial(gather_kernel, n_tp, n_seq, rows),
        out_shape=(
            jax.ShapeDtypeStruct((n_tp * rows, WIDTH), jnp.bfloat16),
            jax.ShapeDtypeStruct((MAXDOC + n_tp * rows, PAIR), jnp.bfloat16),
        ),
        in_specs=[hbm, hbm],
        out_specs=(hbm, hbm),
        scratch_shapes=[
            dma((n_tp,)), dma((n_tp,)), dma((n_tp,)), dma((n_tp,)),
            dma((halo, n_tp)), dma((halo, n_tp)), dma((2,)),
        ],
        compiler_params=pltpu.CompilerParams(collective_id=0, has_side_effects=True),
        name="gather_tokens",
    )(queries, keys_values)


def document_features(starts, ends, first, rows, apart):
    position = first + lax.broadcasted_iota(jnp.int32, (rows, HEAD), 0)
    inside = (position >= starts) & (position < ends)
    if apart:
        return jnp.where(inside, 0.0, APART).astype(jnp.bfloat16)
    return jnp.where(inside, 1.0, 0.0).astype(jnp.bfloat16)


def attend_kernel(base_ref, steps_ref, starts_ref, ends_ref, q_ref, kv_ref, out_ref, key_aug, value_t, query_aug, acc, row_max):
    block = pl.program_id(0)
    base = base_ref[0]
    starts, ends = starts_ref[...], ends_ref[...]
    window_rows = kv_ref.shape[0]

    @pl.when(block == 0)
    def _():
        @pl.loop(0, window_rows // BLOCK)
        def _(i):
            at = pl.multiple_of(i * BLOCK, BLOCK)
            here = pl.ds(at, BLOCK)
            key_aug[here, :HEAD] = kv_ref[here, :HEAD]
            key_aug[here, HEAD:] = document_features(starts, ends, base + at, BLOCK, True)
            value_t[:HEAD, here] = kv_ref[here, HEAD:].astype(jnp.float32).T.astype(jnp.bfloat16)
            value_t[HEAD:, here] = jnp.ones((value_t.shape[0] - HEAD, BLOCK), jnp.bfloat16)

    query_first = base + MAXDOC + block * BLOCK
    features = document_features(starts, ends, query_first, BLOCK, False)
    for h in range(GROUP):
        query_aug[h * BLOCK:(h + 1) * BLOCK, :HEAD] = q_ref[:, h * HEAD:(h + 1) * HEAD]
        query_aug[h * BLOCK:(h + 1) * BLOCK, HEAD:] = features

    def step(index, first):
        at = pl.multiple_of(block * BLOCK + (STEPS - 1 - index) * STEP_KEYS, BLOCK)
        scores = lax.dot_general(
            key_aug[pl.ds(at, STEP_KEYS), :], query_aug[...], (((1,), (1,)), ((), ())),
            preferred_element_type=jnp.float32,
        )
        if first:
            key_pos = lax.broadcasted_iota(jnp.int32, (BLOCK, WIDTH), 0)
            query_pos = lax.broadcasted_iota(jnp.int32, (BLOCK, WIDTH), 1) % BLOCK
            last = jnp.where(key_pos <= query_pos, scores[-BLOCK:], APART)
            scores = jnp.concatenate([scores[:-BLOCK], last], axis=0)
        top = jnp.max(scores, axis=0, keepdims=True) * SCALE
        if not first:
            old = row_max[...]
            top = jnp.maximum(old, top)
            shrink = jnp.exp2(old - top)
        weights = jnp.exp2(scores * SCALE - top).astype(jnp.bfloat16)
        update = jnp.dot(value_t[:, pl.ds(at, STEP_KEYS)], weights, preferred_element_type=jnp.float32)
        row_max[...] = top
        acc[...] = update if first else acc[...] * shrink + update

    step(0, True)

    @pl.loop(1, steps_ref[block])
    def _(index):
        step(index, False)

    result = acc[:HEAD] * (1.0 / acc[HEAD:HEAD + 1])
    for h in range(GROUP):
        out_ref[:, h * HEAD:(h + 1) * HEAD] = result[:, h * BLOCK:(h + 1) * BLOCK].T.astype(jnp.bfloat16)


def attend(base, steps, starts, ends, queries, pairs):
    rows = queries.shape[0]
    window_rows = pairs.shape[0]
    return pl.pallas_call(
        attend_kernel,
        out_shape=jax.ShapeDtypeStruct((rows, WIDTH), jnp.bfloat16),
        grid_spec=pltpu.PrefetchScalarGridSpec(
            num_scalar_prefetch=2,
            grid=(rows // BLOCK,),
            in_specs=[
                pl.BlockSpec((1, HEAD), lambda i, *_: (0, 0)),
                pl.BlockSpec((1, HEAD), lambda i, *_: (0, 0)),
                pl.BlockSpec((BLOCK, WIDTH), lambda i, *_: (i, 0)),
                pl.BlockSpec((window_rows, PAIR), lambda i, *_: (0, 0)),
            ],
            out_specs=pl.BlockSpec((BLOCK, WIDTH), lambda i, *_: (i, 0)),
            scratch_shapes=[
                pltpu.VMEM((window_rows, 2 * HEAD), jnp.bfloat16),
                pltpu.VMEM((HEAD + 16, window_rows), jnp.bfloat16),
                pltpu.VMEM((WIDTH, 2 * HEAD), jnp.bfloat16),
                pltpu.VMEM((HEAD + 16, WIDTH), jnp.float32),
                pltpu.VMEM((1, WIDTH), jnp.float32),
            ],
        ),
        compiler_params=pltpu.CompilerParams(vmem_limit_bytes=48 << 20),
        name="attend_window",
    )(base, steps, starts, ends, queries, pairs)


PIECE_ROWS = 8
PIECE_COLS = 256


def route_kernel(n_seq, order_ref, att_ref, out_ref, middle, outgoing, send1, recv1, send2, recv2, own_sem):
    shard = lax.axis_index("seq")
    slots = att_ref.shape[0]
    halves = WIDTH // PIECE_COLS
    far = ring_order(n_seq)

    barrier = pltpu.get_barrier_semaphore()
    for d in far:
        pl.semaphore_signal(barrier, inc=1, device_id={"seq": lax.rem(shard + d, n_seq)}, device_id_type=MESH)
    pl.semaphore_wait(barrier, n_seq - 1)

    def piece(ref, which):
        return ref.at[
            :,
            pl.ds(pl.multiple_of((which // halves) * PIECE_ROWS, PIECE_ROWS), PIECE_ROWS),
            pl.ds(pl.multiple_of((which % halves) * PIECE_COLS, PIECE_COLS), PIECE_COLS),
        ]

    def group(ref, which):
        return ref.at[pl.ds(which * slots, slots)]

    own = pltpu.make_async_copy(piece(att_ref, shard), group(middle, shard), own_sem.at[0])
    own.start()
    copies = {}
    for d in far:
        peer = lax.rem(shard + d, n_seq)
        copies[d] = pltpu.make_async_remote_copy(
            src_ref=piece(att_ref, peer),
            dst_ref=group(middle, shard),
            send_sem=send1.at[d],
            recv_sem=recv1.at[d],
            device_id={"seq": peer},
            device_id_type=MESH,
        )
        copies[d].start()
    own.wait()
    for d in far:
        copies[d].wait_recv()

    def permute(which):
        for k in range(slots):
            row = which * slots + k
            outgoing[row] = middle[order_ref[row]]

    later = {}
    for d in far:
        peer = lax.rem(shard + d, n_seq)
        permute(peer)
        later[d] = pltpu.make_async_remote_copy(
            src_ref=group(outgoing, peer),
            dst_ref=piece(out_ref, shard),
            send_sem=send2.at[d],
            recv_sem=recv2.at[d],
            device_id={"seq": peer},
            device_id_type=MESH,
        )
        later[d].start()
    permute(shard)
    home = pltpu.make_async_copy(group(outgoing, shard), piece(out_ref, shard), own_sem.at[1])
    home.start()
    home.wait()
    for d in far:
        copies[d].wait_send()
        later[d].wait()


def route(order, attended):
    n_seq = lax.axis_size("seq")
    rows = attended.shape[0]
    slots = rows // BLOCK
    blocks = n_seq * slots
    dma = pltpu.SemaphoreType.DMA
    out = pl.pallas_call(
        functools.partial(route_kernel, n_seq),
        out_shape=jax.ShapeDtypeStruct((slots, BLOCK, WIDTH), jnp.bfloat16),
        in_specs=[pl.BlockSpec(memory_space=pltpu.SMEM), pl.BlockSpec(memory_space=pl.ANY)],
        out_specs=pl.BlockSpec(memory_space=pl.ANY),
        scratch_shapes=[
            pltpu.VMEM((blocks, PIECE_ROWS, PIECE_COLS), jnp.bfloat16),
            pltpu.VMEM((blocks, PIECE_ROWS, PIECE_COLS), jnp.bfloat16),
            dma((n_seq,)), dma((n_seq,)), dma((n_seq,)), dma((n_seq,)), dma((2,)),
        ],
        compiler_params=pltpu.CompilerParams(collective_id=1, has_side_effects=True),
        name="route_blocks",
    )(order, attended.reshape(slots, BLOCK, WIDTH))
    return out.reshape(rows, WIDTH)


def body(queries, keys_values, doc_lengths, block_target):
    n_seq, n_tp = lax.axis_size("seq"), lax.axis_size("tp")
    shard = lax.axis_index("seq")
    shard_rows = n_tp * queries.shape[0]
    slots = shard_rows // BLOCK
    total_blocks = block_target.shape[0]

    ends = jnp.cumsum(doc_lengths)
    starts = ends - doc_lengths
    base = shard * shard_rows - MAXDOC
    firsts = shard * shard_rows + jnp.arange(slots, dtype=jnp.int32) * BLOCK
    first_start = jnp.max(jnp.where(starts[None, :] <= firsts[:, None], starts[None, :], 0), axis=1)
    reach = firsts + BLOCK - first_start
    steps = jnp.minimum((reach + STEP_KEYS - 1) // STEP_KEYS, STEPS).astype(jnp.int32)
    pad = HEAD - starts.shape[0]
    starts_row = jnp.pad(starts, (0, pad), constant_values=1 << 30)[None, :]
    ends_row = jnp.pad(ends, (0, pad), constant_values=1 << 30)[None, :]

    ids = jnp.arange(total_blocks, dtype=jnp.int32)
    earlier = (block_target[None, :] == block_target[:, None]) & (ids[None, :] < ids[:, None])
    place = block_target * slots + jnp.sum(earlier.astype(jnp.int32), axis=1)
    order = jnp.sum(jnp.where(place[None, :] == ids[:, None], ids[None, :], 0), axis=1).astype(jnp.int32)

    q_here, pairs = gather(queries, keys_values)
    attended = attend(base.reshape(1).astype(jnp.int32), steps, starts_row, ends_row, q_here, pairs)
    return route(order, attended)


def solution(mesh):
    placed = (P(("seq", "tp"), None), P(("seq", "tp"), None), P(), P())
    return jax.shard_map(body, mesh=mesh, in_specs=placed, out_specs=P("seq", "tp"), check_vma=False)
```

```python
import functools
import math

import jax
import jax.numpy as jnp
from jax import lax
from jax.experimental import pallas as pl
from jax.experimental.pallas import tpu as pltpu
from jax.sharding import PartitionSpec as P

HEADS = 32
KV_HEADS = 8
HEAD = 128
BLOCK = 128
MAXDOC = 3072

MESH = pl.DeviceIdType.MESH
GROUP = HEADS // KV_HEADS
WIDTH = GROUP * HEAD
PAIR = 2 * HEAD
WINDOW = MAXDOC + BLOCK
TILE = 5 * BLOCK
TILES = WINDOW // TILE
COLS = 2 * HEAD
PIECE_ROWS = 8
PIECE_COLS = 256
ONES = 16
CONTRACT_LAST = (((1,), (1,)), ((), ()))
APART = -32768.0
SCALE = math.log2(math.e) / math.sqrt(HEAD)


def ring_order(n):
    order = []
    for d in range(1, n // 2 + 1):
        order.append(d)
        if n - d != d:
            order.append(n - d)
    return order


def document_features(starts, ends, first, rows, apart):
    position = first + lax.broadcasted_iota(jnp.int32, (rows, HEAD), 0)
    inside = (position >= starts) & (position < ends)
    if apart:
        return jnp.where(inside, 0.0, APART).astype(jnp.bfloat16)
    return jnp.where(inside, 1.0, 0.0).astype(jnp.bfloat16)


def whole_kernel(
    n_tp, n_seq, rows,
    order_ref, starts_ref, ends_ref, q_ref, kv_ref, out_ref,
    pairs, q_here, key_aug, value_t, query_aug, scores_a, scores_b, top_a, top_b, attended, middle, outgoing,
    kv_send, kv_recv, q_send, q_recv, h_send, h_recv, send1, recv1, send2, recv2, own_sem,
):
    me = lax.axis_index("tp")
    shard = lax.axis_index("seq")
    shard_rows = n_tp * rows
    halo = MAXDOC // shard_rows
    slots = shard_rows // BLOCK
    groups = n_tp // 2
    per_group = slots // groups
    my_group = me // 2
    base = shard * shard_rows - MAXDOC
    near = ring_order(n_tp)
    far = ring_order(n_seq)
    starts, ends = starts_ref[...], ends_ref[...]

    barrier = pltpu.get_barrier_semaphore()
    for d in near:
        pl.semaphore_signal(barrier, inc=1, device_id={"tp": lax.rem(me + d, n_tp)}, device_id_type=MESH)
    for d in far:
        pl.semaphore_signal(barrier, inc=1, device_id={"seq": lax.rem(shard + d, n_seq)}, device_id_type=MESH)
    pl.semaphore_wait(barrier, n_tp - 1 + n_seq - 1)

    def columns(ref, which, width):
        return ref.at[:, pl.ds(pl.multiple_of(which * width, width), width)]

    def token_rows(ref, first, which):
        return ref.at[pl.ds(pl.multiple_of(first + which * rows, 64), rows), :]

    own_kv = pltpu.make_async_copy(columns(kv_ref, me, PAIR), token_rows(pairs, MAXDOC, me), own_sem.at[0])
    own_q = pltpu.make_async_copy(columns(q_ref, me, WIDTH), token_rows(q_here, 0, me), own_sem.at[1])
    own_kv.start()
    kv_copies = {}
    for d in near:
        peer = lax.rem(me + d, n_tp)
        kv_copies[d] = pltpu.make_async_remote_copy(
            src_ref=columns(kv_ref, peer, PAIR),
            dst_ref=token_rows(pairs, MAXDOC, me),
            send_sem=kv_send.at[d],
            recv_sem=kv_recv.at[d],
            device_id={"tp": peer},
            device_id_type=MESH,
        )
        kv_copies[d].start()

    def q_copy(peer, send, receive):
        return pltpu.make_async_remote_copy(
            src_ref=columns(q_ref, peer, WIDTH),
            dst_ref=token_rows(q_here, 0, me),
            send_sem=q_send.at[send],
            recv_sem=q_recv.at[receive],
            device_id={"tp": peer},
            device_id_type=MESH,
        )

    own_q.start()
    partner = me + 1 - 2 * (me % 2)
    q_copies = [q_copy(partner, 1, 1)]
    for k in range(1, groups):
        group = lax.rem(my_group + groups - k, groups)
        for i in range(2):
            q_copies.append(q_copy(2 * group + i, 2 * k + i, 2 * k + me % 2))
    for copy in q_copies:
        copy.start()

    @pl.loop(0, pairs.shape[0] // BLOCK)
    def _(i):
        at = pl.multiple_of(i * BLOCK, BLOCK)
        key_aug[pl.ds(at, BLOCK), HEAD:] = document_features(starts, ends, base + at, BLOCK, True)
        value_t[HEAD:, pl.ds(at, BLOCK)] = jnp.ones((ONES, BLOCK), jnp.bfloat16)

    def relay(d, h):
        origin = lax.rem(me + n_tp - d, n_tp)
        return pltpu.make_async_remote_copy(
            src_ref=token_rows(pairs, MAXDOC, origin),
            dst_ref=token_rows(pairs, MAXDOC - h * shard_rows, origin),
            send_sem=h_send.at[h - 1, d],
            recv_sem=h_recv.at[h - 1, d],
            device_id={"seq": lax.rem(shard + h, n_seq)},
            device_id_type=MESH,
        )

    own_kv.wait()
    for h in range(1, halo + 1):
        relay(0, h).start()
    for d in near:
        kv_copies[d].wait_recv()
        for h in range(1, halo + 1):
            relay(d, h).start()

    def prepare(first, count):
        @pl.loop(0, count)
        def _(i):
            at = pl.multiple_of(first + i * BLOCK, BLOCK)
            here = pl.ds(at, BLOCK)
            key_aug[here, :HEAD] = pairs[here, :HEAD]
            value_t[:HEAD, here] = pairs[here, HEAD:].astype(jnp.float32).T.astype(jnp.bfloat16)

    prepare(MAXDOC, slots)
    for h in range(1, halo + 1):
        for d in [0] + near:
            relay(d, h).wait_recv()
        prepare(MAXDOC - h * shard_rows, slots)

    def score_tile(block, local, half, i, scores, top):
        at = pl.multiple_of(block * BLOCK + i * TILE, BLOCK)
        tile = lax.dot_general(
            key_aug[pl.ds(at, TILE), :], query_aug[local, half * COLS:(half + 1) * COLS, :], CONTRACT_LAST,
            preferred_element_type=jnp.float32,
        )
        if i == TILES - 1:
            key_pos = lax.broadcasted_iota(jnp.int32, (BLOCK, COLS), 0)
            query_pos = lax.broadcasted_iota(jnp.int32, (BLOCK, COLS), 1) % BLOCK
            last = jnp.where(key_pos <= query_pos, tile[-BLOCK:], APART)
            tile = jnp.concatenate([tile[:-BLOCK], last], axis=0)
        scores[i * TILE:(i + 1) * TILE, :] = tile
        best = jnp.max(tile.reshape(TILE // 8, 8, COLS), axis=0)
        return best if top is None else jnp.maximum(top, best)

    def weigh_tile(block, i, scores, top, total):
        at = pl.multiple_of(block * BLOCK + i * TILE, BLOCK)
        weights = jnp.exp2(scores[i * TILE:(i + 1) * TILE, :] * SCALE - top).astype(jnp.bfloat16)
        part = jnp.dot(value_t[:, pl.ds(at, TILE)], weights, preferred_element_type=jnp.float32)
        return part if total is None else total + part

    def finish(block, half, total):
        result = total[:HEAD] * (1.0 / total[HEAD:HEAD + 1])
        for h in range(COLS // BLOCK):
            head = result[:, h * BLOCK:(h + 1) * BLOCK].T.reshape(BLOCK // PIECE_ROWS, PIECE_ROWS, HEAD)
            at = half * COLS + h * HEAD
            attended[block, :, :, at:at + HEAD] = head.astype(jnp.bfloat16)

    buffers = ((scores_a, top_a), (scores_b, top_b))

    def overlap(ahead, behind):
        top = None
        if behind is not None:
            block, _, half = behind
            limit = jnp.max(buffers[half][1][...], axis=0, keepdims=True) * SCALE
        total = None
        for i in range(TILES):
            if ahead is not None:
                top = score_tile(*ahead, i, buffers[ahead[2]][0], top)
            if behind is not None:
                total = weigh_tile(block, i, buffers[half][0], limit, total)
        if ahead is not None:
            buffers[ahead[2]][1][...] = top
        if behind is not None:
            finish(block, half, total)

    def piece(which):
        halves = WIDTH // PIECE_COLS
        return which // halves, pl.ds(pl.multiple_of((which % halves) * PIECE_COLS, PIECE_COLS), PIECE_COLS)

    def first_hop(k, d, group):
        peer = lax.rem(shard + d, n_seq)
        row, cols = piece(peer)
        return pltpu.make_async_remote_copy(
            src_ref=attended.at[pl.ds(group * per_group, per_group), row, :, cols],
            dst_ref=middle.at[pl.ds(shard * slots + group * per_group, per_group)],
            send_sem=send1.at[k, d],
            recv_sem=recv1.at[k, d],
            device_id={"seq": peer},
            device_id_type=MESH,
        )

    def own_hop(k, group):
        row, cols = piece(shard)
        return pltpu.make_async_copy(
            attended.at[pl.ds(group * per_group, per_group), row, :, cols],
            middle.at[pl.ds(shard * slots + group * per_group, per_group)],
            own_sem.at[2 + k],
        )

    @pl.loop(0, groups)
    def _(k):
        group = lax.rem(my_group + k, groups)

        @pl.when(k == 0)
        def _():
            own_q.wait()

        @pl.when(k > 0)
        def _():
            q_copy(partner, 2 * k, 2 * k).wait_recv()

        q_copy(partner, 2 * k + 1, 2 * k + 1).wait_recv()
        for local in range(per_group):
            at = pl.multiple_of((group * per_group + local) * BLOCK, BLOCK)
            features = document_features(starts, ends, base + MAXDOC + at, BLOCK, False)
            for h in range(GROUP):
                here = slice(h * BLOCK, (h + 1) * BLOCK)
                query_aug[local, here, :HEAD] = q_here[pl.ds(at, BLOCK), h * HEAD:(h + 1) * HEAD]
                query_aug[local, here, HEAD:] = features

        first = group * per_group
        overlap((first, 0, 0), None)

        @pl.loop(0, per_group - 1)
        def _(local):
            block = first + local
            overlap((block, local, 1), (block, local, 0))
            overlap((block + 1, local + 1, 0), (block, local, 1))

        last = first + per_group - 1
        overlap((last, per_group - 1, 1), (last, per_group - 1, 0))
        overlap(None, (last, per_group - 1, 1))

        own_hop(k, group).start()

        @pl.loop(1, n_seq)
        def _(d):
            first_hop(k, d, group).start()

    @pl.loop(0, groups)
    def _(k):
        own_hop(k, k).wait()

        @pl.loop(1, n_seq)
        def _(d):
            first_hop(k, d, k).wait_recv()

    def permute(which):
        for i in range(slots):
            row = which * slots + i
            outgoing[row] = middle[order_ref[row]]

    def second_hop(d):
        peer = lax.rem(shard + d, n_seq)
        row, cols = piece(shard)
        return pltpu.make_async_remote_copy(
            src_ref=outgoing.at[pl.ds(peer * slots, slots)],
            dst_ref=out_ref.at[:, pl.ds(pl.multiple_of(row * PIECE_ROWS, PIECE_ROWS), PIECE_ROWS), cols],
            send_sem=send2.at[d],
            recv_sem=recv2.at[d],
            device_id={"seq": peer},
            device_id_type=MESH,
        )

    @pl.loop(1, n_seq)
    def _(d):
        permute(lax.rem(shard + d, n_seq))
        second_hop(d).start()

    permute(shard)
    row, cols = piece(shard)
    home = pltpu.make_async_copy(
        outgoing.at[pl.ds(shard * slots, slots)],
        out_ref.at[:, pl.ds(pl.multiple_of(row * PIECE_ROWS, PIECE_ROWS), PIECE_ROWS), cols],
        own_sem.at[0],
    )
    home.start()
    for d in near:
        kv_copies[d].wait_send()
    for copy in q_copies:
        copy.wait_send()
    for h in range(1, halo + 1):
        for d in [0] + near:
            relay(d, h).wait_send()

    @pl.loop(0, groups)
    def _(k):
        @pl.loop(1, n_seq)
        def _(d):
            first_hop(k, d, k).wait_send()

    home.wait()

    @pl.loop(1, n_seq)
    def _(d):
        second_hop(d).wait()


def body(queries, keys_values, doc_lengths, block_target):
    n_seq, n_tp = lax.axis_size("seq"), lax.axis_size("tp")
    rows = queries.shape[0]
    shard_rows = n_tp * rows
    slots = shard_rows // BLOCK
    halo = MAXDOC // shard_rows
    groups = n_tp // 2
    blocks = n_seq * slots
    window_rows = MAXDOC + shard_rows

    ends = jnp.cumsum(doc_lengths)
    starts = ends - doc_lengths
    pad = HEAD - starts.shape[0]
    starts_row = jnp.pad(starts, (0, pad), constant_values=1 << 30)[None, :]
    ends_row = jnp.pad(ends, (0, pad), constant_values=1 << 30)[None, :]

    ids = jnp.arange(blocks, dtype=jnp.int32)
    earlier = (block_target[None, :] == block_target[:, None]) & (ids[None, :] < ids[:, None])
    place = block_target * slots + jnp.sum(earlier.astype(jnp.int32), axis=1)
    order = jnp.sum(jnp.where(place[None, :] == ids[:, None], ids[None, :], 0), axis=1).astype(jnp.int32)

    hbm = pl.BlockSpec(memory_space=pl.ANY)
    vmem = pl.BlockSpec(memory_space=pltpu.VMEM)
    dma = pltpu.SemaphoreType.DMA
    out = pl.pallas_call(
        functools.partial(whole_kernel, n_tp, n_seq, rows),
        out_shape=jax.ShapeDtypeStruct((slots, BLOCK, WIDTH), jnp.bfloat16),
        in_specs=[pl.BlockSpec(memory_space=pltpu.SMEM), vmem, vmem, hbm, hbm],
        out_specs=hbm,
        scratch_shapes=[
            pltpu.VMEM((window_rows, PAIR), jnp.bfloat16),
            pltpu.VMEM((shard_rows, WIDTH), jnp.bfloat16),
            pltpu.VMEM((window_rows, 2 * HEAD), jnp.bfloat16),
            pltpu.VMEM((HEAD + ONES, window_rows), jnp.bfloat16),
            pltpu.VMEM((slots // groups, WIDTH, 2 * HEAD), jnp.bfloat16),
            pltpu.VMEM((WINDOW, COLS), jnp.float32),
            pltpu.VMEM((WINDOW, COLS), jnp.float32),
            pltpu.VMEM((8, COLS), jnp.float32),
            pltpu.VMEM((8, COLS), jnp.float32),
            pltpu.VMEM((slots, BLOCK // PIECE_ROWS, PIECE_ROWS, WIDTH), jnp.bfloat16),
            pltpu.VMEM((blocks, PIECE_ROWS, PIECE_COLS), jnp.bfloat16),
            pltpu.VMEM((blocks, PIECE_ROWS, PIECE_COLS), jnp.bfloat16),
            dma((n_tp,)), dma((n_tp,)), dma((n_tp,)), dma((n_tp,)),
            dma((halo, n_tp)), dma((halo, n_tp)),
            dma((groups, n_seq)), dma((groups, n_seq)), dma((n_seq,)), dma((n_seq,)), dma((2 + groups,)),
        ],
        compiler_params=pltpu.CompilerParams(collective_id=0, has_side_effects=True, vmem_limit_bytes=56 << 20),
        name="attend_and_route",
    )(order, starts_row, ends_row, queries, keys_values)
    return out.reshape(shard_rows, WIDTH)


def solution(mesh):
    placed = (P(("seq", "tp"), None), P(("seq", "tp"), None), P(), P())
    return jax.shard_map(body, mesh=mesh, in_specs=placed, out_specs=P("seq", "tp"), check_vma=False)
```

```python
import functools
import math

import jax
import jax.numpy as jnp
from jax import lax
from jax.experimental import pallas as pl
from jax.experimental.pallas import tpu as pltpu
from jax.sharding import PartitionSpec as P

HEADS = 32
KV_HEADS = 8
HEAD = 128
BLOCK = 128
MAXDOC = 3072

MESH = pl.DeviceIdType.MESH
GROUP = HEADS // KV_HEADS
WIDTH = GROUP * HEAD
PAIR = 2 * HEAD
WINDOW = MAXDOC + BLOCK
TILE = 5 * BLOCK
TILES = WINDOW // TILE
COLS = 2 * HEAD
PIECE_ROWS = 8
PIECE_COLS = 256
ONES = 16
CONTRACT_LAST = (((1,), (1,)), ((), ()))
APART = -32768.0
SCALE = math.log2(math.e) / math.sqrt(HEAD)


def ring_order(n):
    order = []
    for d in range(1, n // 2 + 1):
        order.append(d)
        if n - d != d:
            order.append(n - d)
    return order


def document_features(starts, ends, first, rows, apart):
    position = first + lax.broadcasted_iota(jnp.int32, (rows, HEAD), 0)
    inside = (position >= starts) & (position < ends)
    if apart:
        return jnp.where(inside, 0.0, APART).astype(jnp.bfloat16)
    return jnp.where(inside, 1.0, 0.0).astype(jnp.bfloat16)


def whole_kernel(
    n_tp, n_seq, rows,
    order_ref, starts_ref, ends_ref, q_ref, kv_ref, out_ref,
    pairs, q_here, key_aug, value_t, query_aug, scores_a, scores_b, top_a, top_b, attended, middle, outgoing,
    kv_send, kv_recv, q_send, q_recv, h_send, h_recv, send1, recv1, send2, recv2, own_sem,
):
    me = lax.axis_index("tp")
    shard = lax.axis_index("seq")
    shard_rows = n_tp * rows
    halo = MAXDOC // shard_rows
    slots = shard_rows // BLOCK
    groups = n_tp // 2
    per_group = slots // groups
    my_group = me // 2
    base = shard * shard_rows - MAXDOC
    near = ring_order(n_tp)
    far = ring_order(n_seq)
    starts, ends = starts_ref[...], ends_ref[...]

    barrier = pltpu.get_barrier_semaphore()
    for d in near:
        pl.semaphore_signal(barrier, inc=1, device_id={"tp": lax.rem(me + d, n_tp)}, device_id_type=MESH)
    for d in far:
        pl.semaphore_signal(barrier, inc=1, device_id={"seq": lax.rem(shard + d, n_seq)}, device_id_type=MESH)
    pl.semaphore_wait(barrier, n_tp - 1 + n_seq - 1)

    def columns(ref, which, width):
        return ref.at[:, pl.ds(pl.multiple_of(which * width, width), width)]

    def token_rows(ref, first, which):
        return ref.at[pl.ds(pl.multiple_of(first + which * rows, 64), rows), :]

    own_kv = pltpu.make_async_copy(columns(kv_ref, me, PAIR), token_rows(pairs, MAXDOC, me), own_sem.at[0])
    own_q = pltpu.make_async_copy(columns(q_ref, me, WIDTH), token_rows(q_here, 0, me), own_sem.at[1])
    own_kv.start()
    kv_copies = {}
    for d in near:
        peer = lax.rem(me + d, n_tp)
        kv_copies[d] = pltpu.make_async_remote_copy(
            src_ref=columns(kv_ref, peer, PAIR),
            dst_ref=token_rows(pairs, MAXDOC, me),
            send_sem=kv_send.at[d],
            recv_sem=kv_recv.at[d],
            device_id={"tp": peer},
            device_id_type=MESH,
        )
        kv_copies[d].start()

    def q_copy(peer, send, receive):
        return pltpu.make_async_remote_copy(
            src_ref=columns(q_ref, peer, WIDTH),
            dst_ref=token_rows(q_here, 0, me),
            send_sem=q_send.at[send],
            recv_sem=q_recv.at[receive],
            device_id={"tp": peer},
            device_id_type=MESH,
        )

    partner = me + 1 - 2 * (me % 2)
    q_copies = [q_copy(partner, 1, 1)]
    for k in range(1, groups):
        group = lax.rem(my_group + groups - k, groups)
        for i in range(2):
            q_copies.append(q_copy(2 * group + i, 2 * k + i, 2 * k + me % 2))

    @pl.loop(0, pairs.shape[0] // BLOCK)
    def _(i):
        at = pl.multiple_of(i * BLOCK, BLOCK)
        key_aug[pl.ds(at, BLOCK), HEAD:] = document_features(starts, ends, base + at, BLOCK, True)
        value_t[HEAD:, pl.ds(at, BLOCK)] = jnp.ones((ONES, BLOCK), jnp.bfloat16)

    def relay(d, h):
        origin = lax.rem(me + n_tp - d, n_tp)
        return pltpu.make_async_remote_copy(
            src_ref=token_rows(pairs, MAXDOC, origin),
            dst_ref=token_rows(pairs, MAXDOC - h * shard_rows, origin),
            send_sem=h_send.at[h - 1, d],
            recv_sem=h_recv.at[h - 1, d],
            device_id={"seq": lax.rem(shard + h, n_seq)},
            device_id_type=MESH,
        )

    own_kv.wait()
    for h in range(1, halo + 1):
        relay(0, h).start()
    for i, d in enumerate(near):
        kv_copies[d].wait_recv()
        for h in range(1, halo + 1):
            relay(d, h).start()
        if i == 0:
            own_q.start()
        q_copies[i].start()

    def prepare(first, count):
        @pl.loop(0, count)
        def _(i):
            at = pl.multiple_of(first + i * BLOCK, BLOCK)
            here = pl.ds(at, BLOCK)
            key_aug[here, :HEAD] = pairs[here, :HEAD]
            value_t[:HEAD, here] = pairs[here, HEAD:].astype(jnp.float32).T.astype(jnp.bfloat16)

    prepare(MAXDOC, slots)
    for h in range(1, halo + 1):
        for d in [0] + near:
            relay(d, h).wait_recv()
        prepare(MAXDOC - h * shard_rows, slots)

    def score_tile(block, local, half, i, scores, top):
        at = pl.multiple_of(block * BLOCK + i * TILE, BLOCK)
        tile = lax.dot_general(
            key_aug[pl.ds(at, TILE), :], query_aug[local, half * COLS:(half + 1) * COLS, :], CONTRACT_LAST,
            preferred_element_type=jnp.float32,
        )
        if i == TILES - 1:
            key_pos = lax.broadcasted_iota(jnp.int32, (BLOCK, COLS), 0)
            query_pos = lax.broadcasted_iota(jnp.int32, (BLOCK, COLS), 1) % BLOCK
            last = jnp.where(key_pos <= query_pos, tile[-BLOCK:], APART)
            tile = jnp.concatenate([tile[:-BLOCK], last], axis=0)
        scores[i * TILE:(i + 1) * TILE, :] = tile
        best = jnp.max(tile.reshape(TILE // 8, 8, COLS), axis=0)
        return best if top is None else jnp.maximum(top, best)

    def weigh_tile(block, i, scores, top, total):
        at = pl.multiple_of(block * BLOCK + i * TILE, BLOCK)
        weights = jnp.exp2(scores[i * TILE:(i + 1) * TILE, :] * SCALE - top).astype(jnp.bfloat16)
        part = jnp.dot(value_t[:, pl.ds(at, TILE)], weights, preferred_element_type=jnp.float32)
        return part if total is None else total + part

    def finish(block, half, total):
        result = total[:HEAD] * (1.0 / total[HEAD:HEAD + 1])
        for h in range(COLS // BLOCK):
            head = result[:, h * BLOCK:(h + 1) * BLOCK].T.reshape(BLOCK // PIECE_ROWS, PIECE_ROWS, HEAD)
            at = half * COLS + h * HEAD
            attended[block, :, :, at:at + HEAD] = head.astype(jnp.bfloat16)

    buffers = ((scores_a, top_a), (scores_b, top_b))

    def overlap(ahead, behind):
        top = None
        if behind is not None:
            block, _, half = behind
            limit = jnp.max(buffers[half][1][...], axis=0, keepdims=True) * SCALE
        total = None
        for i in range(TILES):
            if ahead is not None:
                top = score_tile(*ahead, i, buffers[ahead[2]][0], top)
            if behind is not None:
                total = weigh_tile(block, i, buffers[half][0], limit, total)
        if ahead is not None:
            buffers[ahead[2]][1][...] = top
        if behind is not None:
            finish(block, half, total)

    def piece(which):
        halves = WIDTH // PIECE_COLS
        return which // halves, pl.ds(pl.multiple_of((which % halves) * PIECE_COLS, PIECE_COLS), PIECE_COLS)

    def first_hop(k, d, group):
        peer = lax.rem(shard + d, n_seq)
        row, cols = piece(peer)
        return pltpu.make_async_remote_copy(
            src_ref=attended.at[pl.ds(group * per_group, per_group), row, :, cols],
            dst_ref=middle.at[pl.ds(shard * slots + group * per_group, per_group)],
            send_sem=send1.at[k, d],
            recv_sem=recv1.at[k, d],
            device_id={"seq": peer},
            device_id_type=MESH,
        )

    def own_hop(k, group):
        row, cols = piece(shard)
        return pltpu.make_async_copy(
            attended.at[pl.ds(group * per_group, per_group), row, :, cols],
            middle.at[pl.ds(shard * slots + group * per_group, per_group)],
            own_sem.at[2 + k],
        )

    @pl.loop(0, groups)
    def _(k):
        group = lax.rem(my_group + k, groups)

        @pl.when(k == 0)
        def _():
            own_q.wait()

        @pl.when(k > 0)
        def _():
            q_copy(partner, 2 * k, 2 * k).wait_recv()

        q_copy(partner, 2 * k + 1, 2 * k + 1).wait_recv()
        for local in range(per_group):
            at = pl.multiple_of((group * per_group + local) * BLOCK, BLOCK)
            features = document_features(starts, ends, base + MAXDOC + at, BLOCK, False)
            for h in range(GROUP):
                here = slice(h * BLOCK, (h + 1) * BLOCK)
                query_aug[local, here, :HEAD] = q_here[pl.ds(at, BLOCK), h * HEAD:(h + 1) * HEAD]
                query_aug[local, here, HEAD:] = features

        first = group * per_group
        overlap((first, 0, 0), None)

        @pl.loop(0, per_group - 1)
        def _(local):
            block = first + local
            overlap((block, local, 1), (block, local, 0))
            overlap((block + 1, local + 1, 0), (block, local, 1))

        last = first + per_group - 1
        overlap((last, per_group - 1, 1), (last, per_group - 1, 0))
        overlap(None, (last, per_group - 1, 1))

        own_hop(k, group).start()

        @pl.loop(1, n_seq)
        def _(d):
            first_hop(k, d, group).start()

    @pl.loop(0, groups)
    def _(k):
        own_hop(k, k).wait()

        @pl.loop(1, n_seq)
        def _(d):
            first_hop(k, d, k).wait_recv()

    def permute(which):
        for i in range(slots):
            row = which * slots + i
            outgoing[row] = middle[order_ref[row]]

    def second_hop(d):
        peer = lax.rem(shard + d, n_seq)
        row, cols = piece(shard)
        return pltpu.make_async_remote_copy(
            src_ref=outgoing.at[pl.ds(peer * slots, slots)],
            dst_ref=out_ref.at[:, pl.ds(pl.multiple_of(row * PIECE_ROWS, PIECE_ROWS), PIECE_ROWS), cols],
            send_sem=send2.at[d],
            recv_sem=recv2.at[d],
            device_id={"seq": peer},
            device_id_type=MESH,
        )

    @pl.loop(1, n_seq)
    def _(d):
        permute(lax.rem(shard + d, n_seq))
        second_hop(d).start()

    permute(shard)
    row, cols = piece(shard)
    home = pltpu.make_async_copy(
        outgoing.at[pl.ds(shard * slots, slots)],
        out_ref.at[:, pl.ds(pl.multiple_of(row * PIECE_ROWS, PIECE_ROWS), PIECE_ROWS), cols],
        own_sem.at[0],
    )
    home.start()
    for d in near:
        kv_copies[d].wait_send()
    for copy in q_copies:
        copy.wait_send()
    for h in range(1, halo + 1):
        for d in [0] + near:
            relay(d, h).wait_send()

    @pl.loop(0, groups)
    def _(k):
        @pl.loop(1, n_seq)
        def _(d):
            first_hop(k, d, k).wait_send()

    home.wait()

    @pl.loop(1, n_seq)
    def _(d):
        second_hop(d).wait()


def body(queries, keys_values, doc_lengths, block_target):
    n_seq, n_tp = lax.axis_size("seq"), lax.axis_size("tp")
    rows = queries.shape[0]
    shard_rows = n_tp * rows
    slots = shard_rows // BLOCK
    halo = MAXDOC // shard_rows
    groups = n_tp // 2
    blocks = n_seq * slots
    window_rows = MAXDOC + shard_rows

    ends = jnp.cumsum(doc_lengths)
    starts = ends - doc_lengths
    pad = HEAD - starts.shape[0]
    starts_row = jnp.pad(starts, (0, pad), constant_values=1 << 30)[None, :]
    ends_row = jnp.pad(ends, (0, pad), constant_values=1 << 30)[None, :]

    ids = jnp.arange(blocks, dtype=jnp.int32)
    earlier = (block_target[None, :] == block_target[:, None]) & (ids[None, :] < ids[:, None])
    place = block_target * slots + jnp.sum(earlier.astype(jnp.int32), axis=1)
    order = jnp.sum(jnp.where(place[None, :] == ids[:, None], ids[None, :], 0), axis=1).astype(jnp.int32)

    hbm = pl.BlockSpec(memory_space=pl.ANY)
    vmem = pl.BlockSpec(memory_space=pltpu.VMEM)
    dma = pltpu.SemaphoreType.DMA
    out = pl.pallas_call(
        functools.partial(whole_kernel, n_tp, n_seq, rows),
        out_shape=jax.ShapeDtypeStruct((slots, BLOCK, WIDTH), jnp.bfloat16),
        in_specs=[pl.BlockSpec(memory_space=pltpu.SMEM), vmem, vmem, hbm, hbm],
        out_specs=hbm,
        scratch_shapes=[
            pltpu.VMEM((window_rows, PAIR), jnp.bfloat16),
            pltpu.VMEM((shard_rows, WIDTH), jnp.bfloat16),
            pltpu.VMEM((window_rows, 2 * HEAD), jnp.bfloat16),
            pltpu.VMEM((HEAD + ONES, window_rows), jnp.bfloat16),
            pltpu.VMEM((slots // groups, WIDTH, 2 * HEAD), jnp.bfloat16),
            pltpu.VMEM((WINDOW, COLS), jnp.float32),
            pltpu.VMEM((WINDOW, COLS), jnp.float32),
            pltpu.VMEM((8, COLS), jnp.float32),
            pltpu.VMEM((8, COLS), jnp.float32),
            pltpu.VMEM((slots, BLOCK // PIECE_ROWS, PIECE_ROWS, WIDTH), jnp.bfloat16),
            pltpu.VMEM((blocks, PIECE_ROWS, PIECE_COLS), jnp.bfloat16),
            pltpu.VMEM((blocks, PIECE_ROWS, PIECE_COLS), jnp.bfloat16),
            dma((n_tp,)), dma((n_tp,)), dma((n_tp,)), dma((n_tp,)),
            dma((halo, n_tp)), dma((halo, n_tp)),
            dma((groups, n_seq)), dma((groups, n_seq)), dma((n_seq,)), dma((n_seq,)), dma((2 + groups,)),
        ],
        compiler_params=pltpu.CompilerParams(collective_id=0, has_side_effects=True, vmem_limit_bytes=56 << 20),
        name="attend_and_route",
    )(order, starts_row, ends_row, queries, keys_values)
    return out.reshape(shard_rows, WIDTH)


def solution(mesh):
    placed = (P(("seq", "tp"), None), P(("seq", "tp"), None), P(), P())
    return jax.shard_map(body, mesh=mesh, in_specs=placed, out_specs=P("seq", "tp"), check_vma=False)
```

```python
import functools
import math

import jax
import jax.numpy as jnp
from jax import lax
from jax.experimental import pallas as pl
from jax.experimental.pallas import tpu as pltpu
from jax.sharding import PartitionSpec as P

HEADS = 32
KV_HEADS = 8
HEAD = 128
BLOCK = 128
MAXDOC = 3072

MESH = pl.DeviceIdType.MESH
GROUP = HEADS // KV_HEADS
WIDTH = GROUP * HEAD
PAIR = 2 * HEAD
WINDOW = MAXDOC + BLOCK
TILE = 5 * BLOCK
TILES = WINDOW // TILE
COLS = 2 * HEAD
PIECE_ROWS = 8
PIECE_COLS = 128
BATCHES = 2
ONES = 16
CONTRACT_LAST = (((1,), (1,)), ((), ()))
APART = -32768.0
SCALE = math.log2(math.e) / math.sqrt(HEAD)


def ring_order(n):
    order = []
    for d in range(1, n // 2 + 1):
        order.append(d)
        if n - d != d:
            order.append(n - d)
    return order


def document_features(starts, ends, first, rows, apart):
    position = first + lax.broadcasted_iota(jnp.int32, (rows, HEAD), 0)
    inside = (position >= starts) & (position < ends)
    if apart:
        return jnp.where(inside, 0.0, APART).astype(jnp.bfloat16)
    return jnp.where(inside, 1.0, 0.0).astype(jnp.bfloat16)


def whole_kernel(
    n_tp, n_seq, rows,
    order_ref, starts_ref, ends_ref, q_ref, kv_ref, out_ref,
    pairs, q_a, q_b, key_aug, value_t, query_aug, scores_a, scores_b, top_a, top_b, attended_a, attended_b, middle_a, middle_b, outgoing_a, outgoing_b,
    kv_send, kv_recv, q_send, q_recv, h_send, h_recv, send1, recv1, send2, recv2, own_sem,
):
    me = lax.axis_index("tp")
    shard = lax.axis_index("seq")
    shard_rows = n_tp * rows
    halo = MAXDOC // shard_rows
    slots = shard_rows // BLOCK
    groups = n_tp // 2
    per_group = slots // groups
    my_group = me // 2
    q_here = (q_a, q_b)
    base = shard * shard_rows - MAXDOC
    near = ring_order(n_tp)
    far = ring_order(n_seq)

    barrier = pltpu.get_barrier_semaphore()
    for d in near:
        pl.semaphore_signal(barrier, inc=1, device_id={"tp": lax.rem(me + d, n_tp)}, device_id_type=MESH)
    for d in far:
        pl.semaphore_signal(barrier, inc=1, device_id={"seq": lax.rem(shard + d, n_seq)}, device_id_type=MESH)
    pl.semaphore_wait(barrier, n_tp - 1 + n_seq - 1)

    def columns(ref, which, width):
        return ref.at[:, pl.ds(pl.multiple_of(which * width, width), width)]

    def token_rows(ref, first, which):
        return ref.at[pl.ds(pl.multiple_of(first + which * rows, 64), rows), :]

    own_kv = pltpu.make_async_copy(columns(kv_ref, me, PAIR), token_rows(pairs, MAXDOC, me), own_sem.at[0])
    own_kv.start()
    kv_copies = {}
    for d in near:
        peer = lax.rem(me + d, n_tp)
        kv_copies[d] = pltpu.make_async_remote_copy(
            src_ref=columns(kv_ref, peer, PAIR),
            dst_ref=token_rows(pairs, MAXDOC, me),
            send_sem=kv_send.at[d],
            recv_sem=kv_recv.at[d],
            device_id={"tp": peer},
            device_id_type=MESH,
        )
        kv_copies[d].start()

    partner = me + 1 - 2 * (me % 2)

    def kth_group(k):
        beside = my_group + (k % 2) * (1 - 2 * (my_group % 2))
        return lax.rem(beside + 2 * (k // 2), groups)

    def q_copy(batch, peer, send, receive):
        return pltpu.make_async_remote_copy(
            src_ref=q_ref.at[:, pl.ds(pl.multiple_of(peer * WIDTH + batch * COLS, COLS), COLS)],
            dst_ref=q_here[batch].at[pl.ds(pl.multiple_of(me * rows, 64), rows), :],
            send_sem=q_send.at[batch, send],
            recv_sem=q_recv.at[batch, receive],
            device_id={"tp": peer},
            device_id_type=MESH,
        )

    def send_queries(batch, k):
        for i in range(2):
            q_copy(batch, 2 * kth_group(k) + i, 2 * k + i, 2 * k + me % 2).start()

    def own_q(batch):
        return pltpu.make_async_copy(
            q_ref.at[:, pl.ds(pl.multiple_of(me * WIDTH + batch * COLS, COLS), COLS)],
            q_here[batch].at[pl.ds(pl.multiple_of(me * rows, 64), rows), :],
            own_sem.at[1 + batch],
        )

    starts, ends = starts_ref[...], ends_ref[...]

    @pl.loop(0, pairs.shape[0] // BLOCK)
    def _(i):
        at = pl.multiple_of(i * BLOCK, BLOCK)
        key_aug[pl.ds(at, BLOCK), HEAD:] = document_features(starts, ends, base + at, BLOCK, True)
        value_t[HEAD:, pl.ds(at, BLOCK)] = jnp.ones((ONES, BLOCK), jnp.bfloat16)

    def relay(d, h):
        origin = lax.rem(me + n_tp - d, n_tp)
        return pltpu.make_async_remote_copy(
            src_ref=token_rows(pairs, MAXDOC, origin),
            dst_ref=token_rows(pairs, MAXDOC - h * shard_rows, origin),
            send_sem=h_send.at[h - 1, d],
            recv_sem=h_recv.at[h - 1, d],
            device_id={"seq": lax.rem(shard + h, n_seq)},
            device_id_type=MESH,
        )

    own_kv.wait()
    for h in range(1, halo + 1):
        relay(0, h).start()
    for i, d in enumerate(near):
        kv_copies[d].wait_recv()
        for h in range(1, halo + 1):
            relay(d, h).start()
        if i == 1:
            own_q(0).start()
            q_copy(0, partner, 1, 1).start()
        elif i % 2:
            send_queries(0, i // 2)
    send_queries(0, groups - 1)

    def prepare(first, count):
        @pl.loop(0, count)
        def _(i):
            at = pl.multiple_of(first + i * BLOCK, BLOCK)
            here = pl.ds(at, BLOCK)
            key_aug[here, :HEAD] = pairs[here, :HEAD]
            value_t[:HEAD, here] = pairs[here, HEAD:].astype(jnp.float32).T.astype(jnp.bfloat16)

    prepare(MAXDOC, slots)
    for h in range(1, halo + 1):
        for d in [0] + near:
            relay(d, h).wait_recv()
        prepare(MAXDOC - h * shard_rows, slots)

    def score_tile(block, local, i, scores, top):
        at = pl.multiple_of(block * BLOCK + i * TILE, BLOCK)
        tile = lax.dot_general(
            key_aug[pl.ds(at, TILE), :], query_aug[local], CONTRACT_LAST, preferred_element_type=jnp.float32
        )
        if i == TILES - 1:
            key_pos = lax.broadcasted_iota(jnp.int32, (BLOCK, COLS), 0)
            query_pos = lax.broadcasted_iota(jnp.int32, (BLOCK, COLS), 1) % BLOCK
            last = jnp.where(key_pos <= query_pos, tile[-BLOCK:], APART)
            tile = jnp.concatenate([tile[:-BLOCK], last], axis=0)
        scores[i * TILE:(i + 1) * TILE, :] = tile
        best = jnp.max(tile.reshape(TILE // 8, 8, COLS), axis=0)
        return best if top is None else jnp.maximum(top, best)

    def weigh_tile(block, i, scores, top, total):
        at = pl.multiple_of(block * BLOCK + i * TILE, BLOCK)
        weights = jnp.exp2(scores[i * TILE:(i + 1) * TILE, :] * SCALE - top).astype(jnp.bfloat16)
        part = jnp.dot(value_t[:, pl.ds(at, TILE)], weights, preferred_element_type=jnp.float32)
        return part if total is None else total + part

    def finish(batch, block, total):
        result = total[:HEAD] * (1.0 / total[HEAD:HEAD + 1])
        for h in range(COLS // HEAD):
            head = result[:, h * BLOCK:(h + 1) * BLOCK].T.reshape(BLOCK // PIECE_ROWS, PIECE_ROWS, HEAD)
            attended[batch][block, :, :, h * HEAD:(h + 1) * HEAD] = head.astype(jnp.bfloat16)

    buffers = ((scores_a, top_a), (scores_b, top_b))
    middle = (middle_a, middle_b)
    attended = (attended_a, attended_b)
    outgoing = (outgoing_a, outgoing_b)

    def overlap(batch, first, ahead, behind):
        top = total = None
        if behind is not None:
            behind_scores, behind_top = buffers[behind % 2]
            limit = jnp.max(behind_top[...], axis=0, keepdims=True) * SCALE
        for i in range(TILES):
            if ahead is not None:
                top = score_tile(first + ahead, ahead, i, buffers[ahead % 2][0], top)
            if behind is not None:
                total = weigh_tile(first + behind, i, behind_scores, limit, total)
        if ahead is not None:
            buffers[ahead % 2][1][...] = top
        if behind is not None:
            finish(batch, first + behind, total)

    def piece(which):
        parts = COLS // PIECE_COLS
        return which // parts, which % parts

    def piece_of(batch, which, first, count):
        row, col = piece(which)
        cols = pl.ds(pl.multiple_of(col * PIECE_COLS, PIECE_COLS), PIECE_COLS)
        return attended[batch].at[pl.ds(first, count), row, :, cols]

    def first_hop(batch, step, d, first, count):
        peer = lax.rem(shard + d, n_seq)
        return pltpu.make_async_remote_copy(
            src_ref=piece_of(batch, peer, first, count),
            dst_ref=middle[batch].at[pl.ds(shard * slots + first, count)],
            send_sem=send1.at[step, d],
            recv_sem=recv1.at[step, d],
            device_id={"seq": peer},
            device_id_type=MESH,
        )

    def own_hop(batch, step, first, count):
        return pltpu.make_async_copy(
            piece_of(batch, shard, first, count),
            middle[batch].at[pl.ds(shard * slots + first, count)],
            own_sem.at[1 + BATCHES + step],
        )

    def attend_group(batch, k):
        group = kth_group(k)
        first = group * per_group

        @pl.when(k == 0)
        def _():
            own_q(batch).wait()

        @pl.when(k > 0)
        def _():
            q_copy(batch, partner, 2 * k, 2 * k).wait_recv()

        q_copy(batch, partner, 2 * k + 1, 2 * k + 1).wait_recv()
        if batch + 1 < BATCHES:
            @pl.when(k == 0)
            def _():
                own_q(batch + 1).start()
                q_copy(batch + 1, partner, 1, 1).start()

            @pl.when(k > 0)
            def _():
                send_queries(batch + 1, k)

        for local in range(per_group):
            at = pl.multiple_of((first + local) * BLOCK, BLOCK)
            features = document_features(starts, ends, base + MAXDOC + at, BLOCK, False)
            for h in range(COLS // HEAD):
                here = slice(h * BLOCK, (h + 1) * BLOCK)
                query_aug[local, here, :HEAD] = q_here[batch][pl.ds(at, BLOCK), h * HEAD:(h + 1) * HEAD]
                query_aug[local, here, HEAD:] = features

        for unit in range(per_group + 1):
            overlap(batch, first, unit if unit < per_group else None, unit - 1 if unit else None)

    def permute(batch, which):
        for i in range(slots):
            row = which * slots + i
            outgoing[batch][row] = middle[batch][order_ref[row]]

    def out_piece(batch):
        row, col = piece(shard)
        return out_ref.at[
            :,
            pl.ds(pl.multiple_of(row * PIECE_ROWS, PIECE_ROWS), PIECE_ROWS),
            pl.ds(pl.multiple_of(batch * COLS + col * PIECE_COLS, PIECE_COLS), PIECE_COLS),
        ]

    def second_hop(batch, d):
        peer = lax.rem(shard + d, n_seq)
        return pltpu.make_async_remote_copy(
            src_ref=outgoing[batch].at[pl.ds(peer * slots, slots)],
            dst_ref=out_piece(batch),
            send_sem=send2.at[batch, d],
            recv_sem=recv2.at[batch, d],
            device_id={"seq": peer},
            device_id_type=MESH,
        )

    def home(batch):
        return pltpu.make_async_copy(outgoing[batch].at[pl.ds(shard * slots, slots)], out_piece(batch), own_sem.at[0])

    def second_phase(batch):
        @pl.loop(1, n_seq)
        def _(d):
            permute(batch, lax.rem(shard + d, n_seq))
            second_hop(batch, d).start()

        permute(batch, shard)
        home(batch).start()
        home(batch).wait()

    def first_phase(batch, k):
        first = kth_group(k) * per_group
        step = batch * groups + k
        own_hop(batch, step, first, per_group).start()

        @pl.loop(1, n_seq)
        def _(d):
            first_hop(batch, step, d, first, per_group).start()

    def arrived(batch):
        @pl.loop(0, groups)
        def _(k):
            own_hop(batch, batch * groups + k, k * per_group, per_group).wait()

            @pl.loop(1, n_seq)
            def _(d):
                first_hop(batch, batch * groups + k, d, k * per_group, per_group).wait_recv()

    @pl.loop(0, groups)
    def _(k):
        attend_group(0, k)
        first_phase(0, k)

    @pl.loop(0, 1)
    def _(k):
        attend_group(1, k)
        first_phase(1, k)

    arrived(0)
    second_phase(0)

    @pl.loop(1, groups)
    def _(k):
        attend_group(1, k)
        first_phase(1, k)

    arrived(1)
    second_phase(1)

    for d in near:
        kv_copies[d].wait_send()
    for h in range(1, halo + 1):
        for d in [0] + near:
            relay(d, h).wait_send()
    for batch in range(BATCHES):
        for i in range(1, n_tp):
            q_copy(batch, partner, i, i).wait_send()

    @pl.loop(0, groups)
    def _(k):
        @pl.loop(1, n_seq)
        def _(d):
            for batch in range(BATCHES):
                first_hop(batch, batch * groups + k, d, k * per_group, per_group).wait_send()

    @pl.loop(1, n_seq)
    def _(d):
        for batch in range(BATCHES):
            second_hop(batch, d).wait()


def body(queries, keys_values, doc_lengths, block_target):
    n_seq, n_tp = lax.axis_size("seq"), lax.axis_size("tp")
    rows = queries.shape[0]
    shard_rows = n_tp * rows
    slots = shard_rows // BLOCK
    halo = MAXDOC // shard_rows
    groups = n_tp // 2
    blocks = n_seq * slots
    window_rows = MAXDOC + shard_rows

    ends = jnp.cumsum(doc_lengths)
    starts = ends - doc_lengths
    pad = HEAD - starts.shape[0]
    starts_row = jnp.pad(starts, (0, pad), constant_values=1 << 30)[None, :]
    ends_row = jnp.pad(ends, (0, pad), constant_values=1 << 30)[None, :]

    ids = jnp.arange(blocks, dtype=jnp.int32)
    earlier = (block_target[None, :] == block_target[:, None]) & (ids[None, :] < ids[:, None])
    place = block_target * slots + jnp.sum(earlier.astype(jnp.int32), axis=1)
    order = jnp.sum(jnp.where(place[None, :] == ids[:, None], ids[None, :], 0), axis=1).astype(jnp.int32)

    hbm = pl.BlockSpec(memory_space=pl.ANY)
    vmem = pl.BlockSpec(memory_space=pltpu.VMEM)
    dma = pltpu.SemaphoreType.DMA
    out = pl.pallas_call(
        functools.partial(whole_kernel, n_tp, n_seq, rows),
        out_shape=jax.ShapeDtypeStruct((slots, BLOCK, WIDTH), jnp.bfloat16),
        in_specs=[pl.BlockSpec(memory_space=pltpu.SMEM), vmem, vmem, hbm, hbm],
        out_specs=hbm,
        scratch_shapes=[
            pltpu.VMEM((window_rows, PAIR), jnp.bfloat16),
            pltpu.VMEM((shard_rows, COLS), jnp.bfloat16),
            pltpu.VMEM((shard_rows, COLS), jnp.bfloat16),
            pltpu.VMEM((window_rows, 2 * HEAD), jnp.bfloat16),
            pltpu.VMEM((HEAD + ONES, window_rows), jnp.bfloat16),
            pltpu.VMEM((slots // groups, COLS, 2 * HEAD), jnp.bfloat16),
            pltpu.VMEM((WINDOW, COLS), jnp.float32),
            pltpu.VMEM((WINDOW, COLS), jnp.float32),
            pltpu.VMEM((8, COLS), jnp.float32),
            pltpu.VMEM((8, COLS), jnp.float32),
            pltpu.VMEM((slots, BLOCK // PIECE_ROWS, PIECE_ROWS, COLS), jnp.bfloat16),
            pltpu.VMEM((slots, BLOCK // PIECE_ROWS, PIECE_ROWS, COLS), jnp.bfloat16),
            pltpu.VMEM((blocks, PIECE_ROWS, PIECE_COLS), jnp.bfloat16),
            pltpu.VMEM((blocks, PIECE_ROWS, PIECE_COLS), jnp.bfloat16),
            pltpu.VMEM((blocks, PIECE_ROWS, PIECE_COLS), jnp.bfloat16),
            pltpu.VMEM((blocks, PIECE_ROWS, PIECE_COLS), jnp.bfloat16),
            dma((n_tp,)), dma((n_tp,)), dma((BATCHES, n_tp)), dma((BATCHES, n_tp)),
            dma((halo, n_tp)), dma((halo, n_tp)),
            dma((BATCHES * groups, n_seq)), dma((BATCHES * groups, n_seq)), dma((BATCHES, n_seq)), dma((BATCHES, n_seq)),
            dma((2 + BATCHES + BATCHES * groups,)),
        ],
        compiler_params=pltpu.CompilerParams(collective_id=0, has_side_effects=True, vmem_limit_bytes=56 << 20),
        name="attend_and_route",
    )(order, starts_row, ends_row, queries, keys_values)
    return out.reshape(shard_rows, WIDTH)


def solution(mesh):
    placed = (P(("seq", "tp"), None), P(("seq", "tp"), None), P(), P())
    return jax.shard_map(body, mesh=mesh, in_specs=placed, out_specs=P("seq", "tp"), check_vma=False)
```
